256 devices in a mesh: dp: 128 (over z, y, x), col: 2 (over core).
Axes of the slice: x: 4, y: 4, z: 8, core: 2. Of those that a mesh axis runs over, the one named last changes fastest.
Arguments:
- item_owner: int32 [131072, 1], P('dp'), may hold values from 0 to 127; in each aligned block of 1024 rows (0 to 1023, 1024 to 2047, ...) at most 10 rows name the same one
- item_row: int32 [131072], P('dp'), may hold values from 0 to 4095
- seq_lengths: int32 [128, 8], P('dp'), may hold values from 1 to 256, 1024 in all within a row
- table: bfloat16 [524288, 1024], P('dp', 'col'), may hold values from -6 to 6
- w_qkvu: bfloat16 [1024, 4096], P(None, 'col'), may hold values from -0.1875 to 0.1875
- w_out: bfloat16 [1024, 1024], P('col'), may hold values from -0.1875 to 0.1875
Outputs:
- layer_out: bfloat16 [131072, 1024], P('dp', 'col')
The draws below stay inside these ranges and needn't reach their ends.
Inputs may be any that keep to these rules, and one draw needn't show every extreme that they name: `item_owner`: the tokens of one data group name one table shard at most 10 times; in every draw some data group names some shard exactly 10 times. `seq_lengths`: each row sums to 1024; its largest entry is exactly 256.
All inputs are finite; a program needn't handle non-finite values.
Results may differ from the reference program's by a relative error of at most 0.0065.
Values may be sent and summed in bfloat16 or wider, within the bound.
No kernel may reach another device: no remote copies, remote signals or barrier semaphores. Data moves between devices by JAX's collectives and lax.ppermute only.
A program may use at most 64 MiB of HBM per device.

```python
import math
import jax
import jax.numpy as jnp
import numpy as np
from jax import lax

D = 1024
HEADS = 8
DH = 128
TOK_DEV = 1024
SEQS = 8
MAX_LEN = 256
ROWS_DEV = 4096
CAP = 10
ROWS = 524288
TOKENS = 131072
N_DP = 128


def touch_ends(array, stream_key, smallest, top_value):
    longest = array.shape.index(max(array.shape))
    spots = []
    for shift in (0, 1):
        where = [jax.random.randint(jax.random.fold_in(stream_key, axis), (), 0, length) for axis, length in enumerate(array.shape)]
        where[longest] = (where[longest] + shift) % array.shape[longest]
        spots.append(tuple(where))
    return array.at[spots[0]].set(smallest).at[spots[1]].set(top_value)


def steps_of(stream_key, extent, cuts, low, high):
    loudness, own = 1.0, jax.random.fold_in(stream_key, 6)
    for axis_at, blocks in cuts:
        steps = jnp.exp(jax.random.uniform(jax.random.fold_in(own, axis_at), (blocks,), jnp.float32, low / len(cuts), high / len(cuts)))
        loudness = loudness * jnp.repeat(steps, extent[axis_at] // blocks).reshape([-1 if axis == axis_at else 1 for axis in range(len(extent))])
    return loudness


def length_profile(number_of, total, reach, lean):
    loads = [(1 << 20) // math.isqrt(standing ** lean) + 1 for standing in range(2, number_of + 1)]
    surplus, holding = total - reach - (number_of - 1), [1] * (number_of - 1)
    while surplus > 0:
        free = [i for i in range(number_of - 1) if holding[i] < reach]
        whole, left = sum([loads[i] for i in free]), surplus
        for i in free:
            extra = min(reach - holding[i], max(1, left * loads[i] // whole), surplus)
            holding[i] = holding[i] + extra
            surplus = surplus - extra
    return np.array([reach] + holding)


def ragged_sizes(stream_key, amount, total, reach, lean):
    if amount == 2:
        one = jax.random.randint(stream_key, (), max(1, total - reach), min(reach, total - 1) + 1)
        return jnp.stack([one, total - one])
    tallies = jnp.asarray(length_profile(amount, total, reach, lean), jnp.int32)
    couples = (amount - 1) // 2
    giver, taker = tallies[1:1 + 2 * couples:2], tallies[2:2 + 2 * couples:2]
    room = jnp.minimum(giver - 1, reach - taker)
    passed = jax.random.randint(jax.random.fold_in(stream_key, 1), (couples,), 0, 1 << 20) % (room + 1)
    tallies = tallies.at[1:1 + 2 * couples:2].set(giver - passed).at[2:2 + 2 * couples:2].set(taker + passed)
    return tallies[jax.random.permutation(jax.random.fold_in(stream_key, 2), amount)]


def routed_block(own_key, own, number, rows, count, top, reach, lean):
    order = jax.random.permutation(own_key, count)
    packed, usual = shares(count, rows * top, reach, lean, True), shares(count, rows * top, reach, lean, False)
    places = jnp.arange(count)

    def named(sizes, offset_by):
        used = int((sizes > 0).sum())
        fixed = max(1, used // 4)
        moved = fixed + (places - fixed + offset_by * (used - fixed)) % max(1, count - fixed)
        return jnp.zeros((count,), jnp.int32).at[order[jnp.where(places < fixed, places, moved)]].set(jnp.asarray(sizes, jnp.int32))

    sizes = jnp.where(number % 4 == 0, named(packed, number // 4), named(usual, number - number // 4 - 1))
    mixed = jax.random.permutation(jax.random.fold_in(own, 3), count)
    source_of, receiver = mixed[0:count // 2 * 2:2], mixed[1:count // 2 * 2:2]
    slack = jnp.minimum(sizes[source_of] - 1, reach - sizes[receiver]) // 2
    slack = jnp.where((source_of == order[0]) | (receiver == order[0]) | (sizes[receiver] == 0), 0, jnp.maximum(slack, 0))
    moved = jax.random.randint(jax.random.fold_in(own, 4), (count // 2,), 0, 1 << 20) % (slack + 1)
    sizes = sizes.at[source_of].add(-moved).at[receiver].add(moved)
    members = jnp.searchsorted(jnp.cumsum(sizes), jnp.arange(rows * top), side="right").astype(jnp.int32)
    listing = members.reshape(top, rows).T
    listing = listing[jax.random.permutation(jax.random.fold_in(own, 1), rows)]
    offset_by = jax.random.randint(jax.random.fold_in(own, 2), (rows, 1), 0, top)
    return jnp.take_along_axis(listing, (jnp.arange(top)[None, :] + offset_by) % top, axis=1)


def shares(count, total, bound, slope, full):
    weights = [(1 << 20) // math.isqrt(grade ** slope) + 1 for grade in range(1, count + 1)]
    largest = bound if full else min(bound, max(-(-total // count), total * weights[0] // sum(weights)))
    least = 1 if total - largest >= count - 1 else 0
    counts, rest = [largest] + [least] * (count - 1), total - largest - least * (count - 1)
    while rest > 0:
        candidates = [i for i in range(1, count) if counts[i] < largest] or [i for i in range(1, count) if counts[i] < bound]
        whole, remaining = sum([weights[i] for i in candidates]), rest
        for i in candidates:
            more = min(bound - counts[i], max(1, remaining * weights[i] // whole), rest)
            counts[i] = counts[i] + more
            rest = rest - more
    return np.array(counts)


def bell_draw(stream_key, extent, width, bound, cuts=(), dtype=jnp.bfloat16):
    entries = width * jax.random.normal(stream_key, extent, jnp.float32)
    if cuts:
        entries = entries * steps_of(stream_key, extent, cuts, -0.22, 0.18)
    return jnp.clip(entries, -bound, bound).astype(dtype)


def setup_inputs(seed: int = 0) -> dict:
    splits = jax.random.split(jax.random.key(seed), 7)
    item_owner_keys = jax.random.split(jax.random.fold_in(splits[0], 1), TOKENS // TOK_DEV)
    item_owner_turns = jax.random.permutation(jax.random.fold_in(splits[0], 3), TOKENS // TOK_DEV)
    item_owner = jax.vmap(lambda own, number: routed_block(jax.random.fold_in(splits[0], 2), own, number, TOK_DEV, N_DP, 1, CAP, 2))(item_owner_keys, item_owner_turns).reshape((TOKENS, 1))
    item_row = touch_ends(jax.random.randint(splits[1], (TOKENS,), 0, ROWS_DEV), jax.random.fold_in(splits[1], 1), 0, ROWS_DEV - 1).astype(jnp.int32)
    seq_lengths = jax.vmap(lambda own: ragged_sizes(own, SEQS, TOK_DEV, MAX_LEN, 2))(jax.random.split(splits[2], N_DP)).reshape((N_DP, SEQS)).astype(jnp.int32)
    table = bell_draw(splits[3], (ROWS, D), 1.0, 6.0, ((0, 128), (1, 2)))
    w_qkvu = bell_draw(splits[4], (D, 4 * D), D ** -0.5, 0.1875, ((1, 2),))
    w_out = bell_draw(splits[5], (D, D), D ** -0.5, 0.1875, ((0, 2),))
    return {"item_owner": item_owner, "item_row": item_row, "seq_lengths": seq_lengths, "table": table, "w_qkvu": w_qkvu, "w_out": w_out}


def one_group(args, w_qkvu, w_out):
    emb, lengths = args
    proj = jnp.dot(emb, w_qkvu, preferred_element_type=jnp.float32)
    qkvu = jax.nn.silu(proj).astype(jnp.bfloat16).reshape(TOK_DEV, HEADS, 4, DH)
    query = qkvu[:, :, 0, :].astype(jnp.float32)
    keys = qkvu[:, :, 1, :].astype(jnp.float32)
    values = qkvu[:, :, 2, :].astype(jnp.float32)
    gates = qkvu[:, :, 3, :].astype(jnp.float32).reshape(TOK_DEV, D)
    ends = jnp.cumsum(lengths)
    position = jnp.arange(TOK_DEV)
    segment = lax.optimization_barrier(jnp.sum((ends[None, :] <= position[:, None]).astype(jnp.int32), axis=1))
    visible = (segment[:, None] == segment[None, :]) & (position[None, :] <= position[:, None])
    scores = jnp.einsum('qhd,khd->hqk', query, keys) / jnp.sqrt(jnp.float32(DH))
    weights = jnp.where(visible[None], jax.nn.silu(scores), 0.0) / MAX_LEN
    weights = weights.astype(jnp.bfloat16).astype(jnp.float32)
    attn = jnp.einsum('hqk,khd->qhd', weights, values).reshape(TOK_DEV, D)
    mean = lax.optimization_barrier(jnp.mean(attn, axis=1, keepdims=True))
    msq = lax.optimization_barrier(jnp.mean(attn * attn, axis=1, keepdims=True))
    normed = (attn - mean) / jnp.sqrt(msq - mean * mean + 1e-05)
    hidden = (normed * gates).astype(jnp.bfloat16)
    mixed = jnp.dot(hidden, w_out, preferred_element_type=jnp.float32)
    return (emb.astype(jnp.float32) + mixed).astype(jnp.bfloat16)

def reference(item_owner, item_row, seq_lengths, table, w_qkvu, w_out):
    ids = (item_owner[:, 0] * ROWS_DEV + item_row).astype(jnp.int32)
    emb = jnp.take(table, ids, axis=0).reshape(N_DP, TOK_DEV, D)
    result = lax.map(lambda args: one_group(args, w_qkvu, w_out), (emb, seq_lengths))
    return result.reshape(N_DP * TOK_DEV, D)
```

```python
import jax
import jax.numpy as jnp
from jax import lax
from jax.experimental import pallas as pl
from jax.experimental.pallas import tpu as pltpu
from jax.sharding import PartitionSpec as P

D = 1024
DH = 128
MAX_LEN = 256
TOK = 1024
HALF = 512
CAP = 10
WIN = HALF + MAX_LEN
LOCAL = 4
F32 = jnp.float32
BF16 = jnp.bfloat16
NT = (((1,), (1,)), ((), ()))


def route_kernel(owner_ref, row_ref, wanted_ref, dest_ref):
    sub = lax.broadcasted_iota(jnp.int32, (128, 128), 0)
    lane = lax.broadcasted_iota(jnp.int32, (128, 128), 1)
    before = (sub < lane).astype(F32).astype(BF16)
    count = jnp.zeros((128, 1), F32)
    high = jnp.zeros((128, 128), F32)
    low = jnp.zeros((128, 128), F32)
    for b in range(TOK // 128):
        owner = owner_ref[b : b + 1, :]
        row = row_ref[b : b + 1, :]
        hit = (sub == owner).astype(F32)
        hit16 = hit.astype(BF16)
        rank = jnp.dot(hit16, before, preferred_element_type=F32) + count
        slot = jnp.sum(hit * rank, axis=0, keepdims=True).astype(jnp.int32)
        count = count + jnp.sum(hit, axis=1, keepdims=True)
        dest_ref[b : b + 1, :] = owner * CAP + slot
        here = sub == slot
        top = (row >> 6).astype(F32)
        rest = (row & 63).astype(F32)
        high += lax.dot_general(
            hit16, jnp.where(here, top, 0.0).astype(BF16), NT, preferred_element_type=F32
        )
        low += lax.dot_general(
            hit16, jnp.where(here, rest, 0.0).astype(BF16), NT, preferred_element_type=F32
        )
    wanted_ref[...] = (high * 64.0 + low).astype(jnp.int32)


def route(owner, row):
    return pl.pallas_call(
        route_kernel,
        out_shape=(
            jax.ShapeDtypeStruct((128, 128), jnp.int32),
            jax.ShapeDtypeStruct((8, 128), jnp.int32),
        ),
        name="route",
    )(owner.reshape(8, 128), row.reshape(8, 128))


def pick_kernel(dest_ref, arrived_ref, out_ref):
    wide = lax.broadcasted_iota(jnp.int32, (256, 128 * CAP), 1)
    for b in range(WIN // 256):
        hit = (dest_ref[b * 256 : (b + 1) * 256, :] == wide).astype(F32).astype(BF16)
        out_ref[b * 256 : (b + 1) * 256, :] = jnp.dot(
            hit, arrived_ref[...], preferred_element_type=F32
        ).astype(BF16)


def pick(dest, arrived):
    return pl.pallas_call(
        pick_kernel,
        out_shape=jax.ShapeDtypeStruct((WIN, HALF), BF16),
        cost_estimate=pl.CostEstimate(
            flops=2 * WIN * 1280 * HALF, bytes_accessed=3 << 20, transcendentals=0
        ),
        name="pick",
    )(dest, arrived)


def layer_kernel(
    place_ref,
    dest_ref,
    arrived_ref,
    mine_ref,
    wq0_hbm,
    wq1_hbm,
    wo0_hbm,
    wo1_hbm,
    keep_ref,
    send_ref,
    w_ref,
    wo_ref,
    emb_ref,
    mask_ref,
    attn_ref,
    gate_ref,
    sems,
):
    c = place_ref[0]
    copies = []
    for part, src in enumerate((wq0_hbm, wq1_hbm)):
        for h in range(LOCAL):
            n = part * LOCAL + h
            copies.append(
                pltpu.make_async_copy(src.at[:, pl.ds(h * 512, 512)], w_ref.at[n], sems.at[n])
            )
    for part, src in enumerate((wo0_hbm, wo1_hbm)):
        copies.append(pltpu.make_async_copy(src, wo_ref.at[part], sems.at[8 + part]))
    for cp in copies:
        cp.start()

    mine = pl.multiple_of(c * HALF, HALF)
    other = pl.multiple_of(HALF - c * HALF, HALF)
    wide = lax.broadcasted_iota(jnp.int32, (256, 128 * CAP), 1)
    for b in range(WIN // 256):
        at = slice(b * 256, (b + 1) * 256)
        hit = (dest_ref[at, :] == wide).astype(F32).astype(BF16)
        emb_ref[at, pl.ds(other, HALF)] = jnp.dot(
            hit, arrived_ref[...], preferred_element_type=F32
        ).astype(BF16)
        emb_ref[at, pl.ds(mine, HALF)] = mine_ref[at, :]

    base = c * HALF - MAX_LEN
    for b in range(2):
        q = lax.broadcasted_iota(jnp.int32, (256, 512), 0) + (base + 256 * (b + 1))
        k = lax.broadcasted_iota(jnp.int32, (256, 512), 1) + (base + 256 * b)
        first = jnp.zeros((256, 512), jnp.int32)
        end = jnp.int32(0)
        for s in range(8):
            end = end + place_ref[1 + s]
            first = jnp.where(q >= end, end, first)
        ok = (k >= first) & (k <= q)
        mask_ref[b] = jnp.where(ok, F32(1.0 / MAX_LEN), F32(0.0))

    scale = F32(0.5 / (DH**0.5))

    def silu(x):
        h = x * F32(0.5)
        return h * (F32(1.0) + jnp.tanh(h))

    for n in range(8):
        copies[n].wait()
        w = w_ref.at[n]
        kv = silu(
            jnp.dot(emb_ref[...], w[:, DH : 3 * DH], preferred_element_type=F32)
        ).astype(BF16)
        own = emb_ref[MAX_LEN:, :]
        q = silu(jnp.dot(own, w[:, :DH], preferred_element_type=F32)).astype(BF16)
        gate_ref[:, n * DH : (n + 1) * DH] = silu(
            jnp.dot(own, w[:, 3 * DH :], preferred_element_type=F32)
        ).astype(BF16)
        for b in range(2):
            ks = kv[b * 256 : b * 256 + 512, :DH]
            vs = kv[b * 256 : b * 256 + 512, DH:]
            s = lax.dot_general(
                q[b * 256 : (b + 1) * 256], ks, NT, preferred_element_type=F32
            )
            h = s * scale
            p = (h * (F32(1.0) + jnp.tanh(h)) * mask_ref[b]).astype(BF16)
            attn_ref[b * 256 : (b + 1) * 256, n * DH : (n + 1) * DH] = jnp.dot(
                p, vs, preferred_element_type=F32
            )
    copies[8].wait()
    copies[9].wait()
    for b in range(2):
        at = slice(b * 256, (b + 1) * 256)
        attn = attn_ref[at, :]
        mean = jnp.sum(attn, axis=1, keepdims=True) * F32(1.0 / D)
        msq = jnp.sum(attn * attn, axis=1, keepdims=True) * F32(1.0 / D)
        scale_row = lax.rsqrt(msq - mean * mean + F32(1e-05))
        hidden = ((attn - mean) * scale_row * gate_ref[at, :].astype(F32)).astype(BF16)
        rows = slice(MAX_LEN + b * 256, MAX_LEN + (b + 1) * 256)
        for where, out_ref in ((other, send_ref), (mine, keep_ref)):
            mixed = jnp.dot(
                hidden[:, :HALF], wo_ref[0, :, pl.ds(where, HALF)], preferred_element_type=F32
            ) + jnp.dot(
                hidden[:, HALF:], wo_ref[1, :, pl.ds(where, HALF)], preferred_element_type=F32
            )
            out_ref[at, :] = (emb_ref[rows, pl.ds(where, HALF)].astype(F32) + mixed).astype(BF16)


def layer(place, dest, arrived, mine, wq0, wq1, wo0, wo1):
    vmem = pl.BlockSpec(memory_space=pltpu.VMEM)
    anywhere = pl.BlockSpec(memory_space=pl.ANY)
    return pl.pallas_call(
        layer_kernel,
        out_shape=(
            jax.ShapeDtypeStruct((HALF, HALF), BF16),
            jax.ShapeDtypeStruct((HALF, HALF), BF16),
        ),
        in_specs=[pl.BlockSpec(memory_space=pltpu.SMEM), vmem, vmem, vmem] + [anywhere] * 4,
        out_specs=(vmem, vmem),
        scratch_shapes=[
            pltpu.VMEM((8, D, 512), BF16),
            pltpu.VMEM((2, HALF, D), BF16),
            pltpu.VMEM((WIN, D), BF16),
            pltpu.VMEM((2, 256, 512), F32),
            pltpu.VMEM((HALF, D), F32),
            pltpu.VMEM((HALF, D), BF16),
            pltpu.SemaphoreType.DMA((10,)),
        ],
        compiler_params=pltpu.CompilerParams(vmem_limit_bytes=40 << 20),
        cost_estimate=pl.CostEstimate(
            flops=9 << 30, bytes_accessed=16 << 20, transcendentals=5 << 20
        ),
        name="layer",
    )(place, dest, arrived, mine, wq0, wq1, wo0, wo1)


def local(item_owner, item_row, seq_lengths, table, w_qkvu, w_out):
    c = lax.axis_index("col")
    swap = [(0, 1), (1, 0)]
    wanted, dest = route(item_owner, item_row)
    asked = lax.all_to_all(wanted[:, None, :], "dp", 0, 0, tiled=True)
    rows = asked[:, 0, :CAP].reshape(128 * CAP)
    fetched = table.at[rows].get(mode="promise_in_bounds")
    arrived = lax.all_to_all(fetched.reshape(128, 4 * CAP, 128), "dp", 0, 0, tiled=True)
    wq1 = lax.ppermute(w_qkvu, "col", swap)
    wo1 = lax.ppermute(w_out, "col", swap)
    padded = jnp.concatenate([jnp.full((MAX_LEN,), -1, jnp.int32), dest.reshape(TOK)])
    window = lax.dynamic_slice(padded, (c * HALF,), (WIN,)).reshape(WIN, 1)
    place = jnp.concatenate([jnp.full((1,), c, jnp.int32), seq_lengths[0]])
    theirs = lax.ppermute(arrived, "col", swap).reshape(128 * CAP, HALF)
    mine = pick(window, arrived.reshape(128 * CAP, HALF))
    keep, send = layer(place, window, theirs, mine, w_qkvu, wq1, w_out, wo1)
    got = lax.ppermute(send, "col", swap)
    first = jnp.where(c == 0, keep, got)
    second = jnp.where(c == 0, got, keep)
    return jnp.concatenate([first, second], axis=0)


def solution(mesh):
    return jax.shard_map(
        local,
        mesh=mesh,
        in_specs=(
            P("dp", None),
            P("dp"),
            P("dp", None),
            P("dp", "col"),
            P(None, "col"),
            P("col", None),
        ),
        out_specs=P("dp", "col"),
        check_vma=False,
    )
```

```python
import jax
import jax.numpy as jnp
from jax import lax
from jax.experimental import pallas as pl
from jax.experimental.pallas import tpu as pltpu
from jax.sharding import PartitionSpec as P

D = 1024
DH = 128
MAX_LEN = 256
TOK = 1024
HALF = 512
CAP = 10
WIN = HALF + MAX_LEN
LOCAL = 4
F32 = jnp.float32
BF16 = jnp.bfloat16
NT = (((1,), (1,)), ((), ()))


def route_kernel(owner_ref, row_ref, wanted_ref, dest_ref):
    sub = lax.broadcasted_iota(jnp.int32, (128, 128), 0)
    lane = lax.broadcasted_iota(jnp.int32, (128, 128), 1)
    before = (sub < lane).astype(F32).astype(BF16)
    count = jnp.zeros((128, 1), F32)
    high = jnp.zeros((128, 128), F32)
    low = jnp.zeros((128, 128), F32)
    for b in range(TOK // 128):
        owner = owner_ref[b : b + 1, :]
        row = row_ref[b : b + 1, :]
        hit = (sub == owner).astype(F32)
        hit16 = hit.astype(BF16)
        rank = jnp.dot(hit16, before, preferred_element_type=F32) + count
        slot = jnp.sum(hit * rank, axis=0, keepdims=True).astype(jnp.int32)
        count = count + jnp.sum(hit, axis=1, keepdims=True)
        dest_ref[b : b + 1, :] = owner * CAP + slot
        here = sub == slot
        spot = ((row >> 3) << 5) + (row & 7)
        top = (spot >> 6).astype(F32)
        rest = (spot & 63).astype(F32)
        high += lax.dot_general(
            hit16, jnp.where(here, top, 0.0).astype(BF16), NT, preferred_element_type=F32
        )
        low += lax.dot_general(
            hit16, jnp.where(here, rest, 0.0).astype(BF16), NT, preferred_element_type=F32
        )
    wanted_ref[...] = (high * 64.0 + low).astype(jnp.int32)


def route(owner, row):
    return pl.pallas_call(
        route_kernel,
        out_shape=(
            jax.ShapeDtypeStruct((128, 128), jnp.int32),
            jax.ShapeDtypeStruct((8, 128), jnp.int32),
        ),
        name="route",
    )(owner.reshape(8, 128), row.reshape(8, 128))


def fetch_kernel(asked_ref, table_ref, out_ref, tall_ref, wide_ref):
    def widen(j, _):
        at = pl.ds(pl.multiple_of(j * 16, 16), 16)
        for k in range(4):
            v = table_ref[at, k * 128 : (k + 1) * 128].astype(F32)
            tall_ref[pl.ds(pl.multiple_of(j * 64 + k * 8, 8), 8), :] = v[:8]
            tall_ref[pl.ds(pl.multiple_of(j * 64 + 32 + k * 8, 8), 8), :] = v[8:]
        return 0

    lax.fori_loop(0, 4096 // 16, widen, 0, unroll=4)

    def body(g, _):
        for s in range(CAP):
            at = asked_ref[g, s]
            wide_ref[pl.ds(g * 40 + 4 * s, 4), :] = tall_ref[pl.ds(at, 4, stride=8), :]
        return 0

    lax.fori_loop(0, 128, body, 0, unroll=2)
    out_ref[...] = wide_ref[...].astype(BF16)


def fetch(asked, table):
    return pl.pallas_call(
        fetch_kernel,
        out_shape=jax.ShapeDtypeStruct((128 * 40, 128), BF16),
        in_specs=[
            pl.BlockSpec(memory_space=pltpu.SMEM),
            pl.BlockSpec(memory_space=pltpu.VMEM),
        ],
        out_specs=pl.BlockSpec(memory_space=pltpu.VMEM),
        scratch_shapes=[
            pltpu.VMEM((4096 * 4, 128), F32),
            pltpu.VMEM((128 * 40, 128), F32),
        ],
        compiler_params=pltpu.CompilerParams(vmem_limit_bytes=18 << 20),
        name="fetch",
    )(asked, table)


def place_kernel(
    place_ref, dest_ref, arrived_ref, w_hbm, mine_ref, send_ref, held_hbm, wide_ref, emb_ref
):
    wide_ref[...] = arrived_ref[...].astype(F32)

    def body(j, _):
        for r in range(8):
            at = dest_ref[j * 8 + r]
            emb_ref[pl.ds(MAX_LEN * 4 + j * 32 + r, 4, stride=8), :] = wide_ref[
                pl.ds(pl.multiple_of(at * 4, 4), 4), :
            ]
        return 0

    lax.fori_loop(0, TOK // 8, body, 0, unroll=2)
    emb_ref[: MAX_LEN * 4, :] = jnp.zeros((MAX_LEN * 4, 128), F32)
    c = place_ref[0]

    def window(out_ref, base):
        def body(m, _):
            rows = pl.ds(pl.multiple_of(m * 16, 16), 16)
            for k in range(4):
                lo = emb_ref[pl.ds(pl.multiple_of(base + m * 64 + k * 8, 8), 8), :]
                hi = emb_ref[pl.ds(pl.multiple_of(base + m * 64 + 32 + k * 8, 8), 8), :]
                out_ref[rows, k * 128 : (k + 1) * 128] = jnp.concatenate(
                    [lo, hi], axis=0
                ).astype(BF16)
            return 0

        lax.fori_loop(0, WIN // 16, body, 0, unroll=4)

    window(send_ref, pl.multiple_of((1 - c) * HALF * 4, HALF * 4))
    window(mine_ref, pl.multiple_of(c * HALF * 4, HALF * 4))


def put(place, dest, arrived, w):
    vmem = pl.BlockSpec(memory_space=pltpu.VMEM)
    smem = pl.BlockSpec(memory_space=pltpu.SMEM)
    return pl.pallas_call(
        place_kernel,
        out_shape=(
            jax.ShapeDtypeStruct((WIN, HALF), BF16),
            jax.ShapeDtypeStruct((WIN, HALF), BF16),
            jax.ShapeDtypeStruct((D, 4 * HALF), BF16),
        ),
        in_specs=[smem, smem, vmem, pl.BlockSpec(memory_space=pltpu.HBM)],
        out_specs=(vmem, vmem, pl.BlockSpec(memory_space=pltpu.HBM)),
        input_output_aliases={3: 2},
        scratch_shapes=[
            pltpu.VMEM((128 * 40, 128), F32),
            pltpu.VMEM(((TOK + MAX_LEN) * 4, 128), F32),
        ],
        compiler_params=pltpu.CompilerParams(vmem_limit_bytes=12 << 20),
        name="put",
    )(place, dest, arrived, w)


def silu(x):
    h = x * F32(0.5)
    return h * (F32(1.0) + jnp.tanh(h))


def layer_kernel(
    place_ref,
    lengths_ref,
    mine_ref,
    theirs_ref,
    wq0_ref,
    wq1_hbm,
    wo0_hbm,
    wo1_hbm,
    send_ref,
    hidden_ref,
    kv_ref,
    qu_ref,
    emb_ref,
    w_ref,
    wo_ref,
    mask_ref,
    attn_ref,
    gate_ref,
    sems,
):
    c = place_ref[0]
    other = pl.multiple_of(HALF - c * HALF, HALF)
    copies = [
        pltpu.make_async_copy(
            wq1_hbm.at[:, pl.ds(h * 512, 512)], w_ref.at[h], sems.at[h]
        )
        for h in range(LOCAL)
    ]
    for part, src in enumerate((wo0_hbm, wo1_hbm)):
        copies.append(
            pltpu.make_async_copy(
                src.at[:, pl.ds(other, HALF)],
                wo_ref.at[pl.ds(part * HALF, HALF)],
                sems.at[LOCAL + part],
            )
        )
    for cp in copies:
        cp.start()

    @pl.when(c == 0)
    def _():
        emb_ref[:, :HALF] = mine_ref[...]
        emb_ref[:, HALF:] = theirs_ref[...]

    @pl.when(c != 0)
    def _():
        emb_ref[:, :HALF] = theirs_ref[...]
        emb_ref[:, HALF:] = mine_ref[...]

    base = c * HALF - MAX_LEN
    for b in range(2):
        q = lax.broadcasted_iota(jnp.int32, (256, 1), 0) + (base + 256 * (b + 1))
        k = lax.broadcasted_iota(jnp.int32, (256, 512), 1) + (base + 256 * b)
        first = jnp.zeros((256, 1), jnp.int32)
        end = jnp.int32(0)
        for s in range(8):
            end = end + lengths_ref[0, s]
            first = jnp.where(q >= end, end, first)
        ok = (k >= first) & (k <= q)
        mask_ref[b] = jnp.where(ok, F32(1.0 / MAX_LEN), F32(0.0))

    scale = F32(0.5 / (DH**0.5))
    def attend(n, qu, kv):
        for b in range(2):
            ks = kv[b * 256 : b * 256 + 512, :DH]
            vs = kv[b * 256 : b * 256 + 512, DH:]
            s = lax.dot_general(
                qu[b * 256 : (b + 1) * 256, :DH], ks, NT, preferred_element_type=F32
            )
            h = s * scale
            p = (h * (F32(1.0) + jnp.tanh(h)) * mask_ref[b]).astype(BF16)
            attn_ref[b * 256 : (b + 1) * 256, n * DH : (n + 1) * DH] = jnp.dot(
                p, vs, preferred_element_type=F32
            )

    for n in range(9):
        if n < 8:
            if n < LOCAL:
                w = wq0_ref.at[:, n * 512 : (n + 1) * 512]
            else:
                copies[n - LOCAL].wait()
                w = w_ref.at[n - LOCAL]
            kv_ref[n % 2] = silu(
                jnp.dot(emb_ref[...], w[:, DH : 3 * DH], preferred_element_type=F32)
            ).astype(BF16)
        if n > 0:
            attend(n - 1, qu_ref[(n - 1) % 2], kv_ref[(n - 1) % 2])
        if n < 8:
            ends = jnp.concatenate([w[:, :DH], w[:, 3 * DH :]], axis=1)
            qu = silu(
                jnp.dot(emb_ref[MAX_LEN:, :], ends, preferred_element_type=F32)
            ).astype(BF16)
            qu_ref[n % 2] = qu
            gate_ref[:, n * DH : (n + 1) * DH] = qu[:, DH:]
    copies[LOCAL].wait()
    copies[LOCAL + 1].wait()
    for b in range(2):
        at = slice(b * 256, (b + 1) * 256)
        attn = attn_ref[at, :]
        mean = jnp.sum(attn, axis=1, keepdims=True) * F32(1.0 / D)
        msq = jnp.sum(attn * attn, axis=1, keepdims=True) * F32(1.0 / D)
        scale_row = lax.rsqrt(msq - mean * mean + F32(1e-05))
        hidden = ((attn - mean) * scale_row * gate_ref[at, :].astype(F32)).astype(BF16)
        hidden_ref[at, :] = hidden
        mixed = jnp.dot(hidden, wo_ref[...], preferred_element_type=F32)
        emb = theirs_ref[MAX_LEN + b * 256 : MAX_LEN + (b + 1) * 256, :].astype(F32)
        send_ref[at, :] = (emb + mixed).astype(BF16)


def layer(place, lengths, mine, theirs, wq0, wq1, wo0, wo1):
    vmem = pl.BlockSpec(memory_space=pltpu.VMEM)
    hbm = pl.BlockSpec(memory_space=pltpu.HBM)
    smem = pl.BlockSpec(memory_space=pltpu.SMEM)
    return pl.pallas_call(
        layer_kernel,
        out_shape=(
            jax.ShapeDtypeStruct((HALF, HALF), BF16),
            jax.ShapeDtypeStruct((HALF, D), BF16),
        ),
        in_specs=[smem, smem, vmem, vmem, vmem] + [hbm] * 3,
        out_specs=(vmem, vmem),
        scratch_shapes=[
            pltpu.VMEM((2, WIN, 256), BF16),
            pltpu.VMEM((2, HALF, 256), BF16),
            pltpu.VMEM((WIN, D), BF16),
            pltpu.VMEM((LOCAL, D, 512), BF16),
            pltpu.VMEM((D, HALF), BF16),
            pltpu.VMEM((2, 256, 512), F32),
            pltpu.VMEM((HALF, D), F32),
            pltpu.VMEM((HALF, D), BF16),
            pltpu.SemaphoreType.DMA((LOCAL + 2,)),
        ],
        compiler_params=pltpu.CompilerParams(vmem_limit_bytes=30 << 20),
        cost_estimate=pl.CostEstimate(
            flops=7 << 30, bytes_accessed=12 << 20, transcendentals=5 << 20
        ),
        name="layer",
    )(place, lengths, mine, theirs, wq0, wq1, wo0, wo1)


def keep_kernel(
    place_ref, hidden_ref, mine_ref, wo0_hbm, wo1_hbm, out_hbm, wo_ref, out_ref, sems
):
    mine = pl.multiple_of(place_ref[0] * HALF, HALF)
    copies = [
        pltpu.make_async_copy(
            src.at[:, pl.ds(mine, HALF)], wo_ref.at[pl.ds(part * HALF, HALF)], sems.at[part]
        )
        for part, src in enumerate((wo0_hbm, wo1_hbm))
    ]
    for cp in copies:
        cp.start()
    for cp in copies:
        cp.wait()
    mixed = jnp.dot(hidden_ref[...], wo_ref[...], preferred_element_type=F32)
    out_ref[...] = (mine_ref[MAX_LEN:, :].astype(F32) + mixed).astype(BF16)
    done = pltpu.make_async_copy(out_ref, out_hbm.at[pl.ds(mine, HALF), :], sems.at[2])
    done.start()
    done.wait()


def keep(place, hidden, mine, wo0, wo1):
    vmem = pl.BlockSpec(memory_space=pltpu.VMEM)
    hbm = pl.BlockSpec(memory_space=pltpu.HBM)
    return pl.pallas_call(
        keep_kernel,
        out_shape=jax.ShapeDtypeStruct((TOK, HALF), BF16),
        in_specs=[pl.BlockSpec(memory_space=pltpu.SMEM), vmem, vmem, hbm, hbm],
        out_specs=hbm,
        scratch_shapes=[
            pltpu.VMEM((D, HALF), BF16),
            pltpu.VMEM((HALF, HALF), BF16),
            pltpu.SemaphoreType.DMA((3,)),
        ],
        compiler_params=pltpu.CompilerParams(vmem_limit_bytes=10 << 20),
        cost_estimate=pl.CostEstimate(
            flops=1 << 29, bytes_accessed=3 << 20, transcendentals=0
        ),
        name="keep",
    )(place, hidden, mine, wo0, wo1)


def join_kernel(place_ref, got_ref, half_hbm, out_hbm, sem):
    other = pl.multiple_of(HALF - place_ref[0] * HALF, HALF)
    done = pltpu.make_async_copy(got_ref, out_hbm.at[pl.ds(other, HALF), :], sem)
    done.start()
    done.wait()


def join(place, got, half):
    hbm = pl.BlockSpec(memory_space=pltpu.HBM)
    return pl.pallas_call(
        join_kernel,
        out_shape=jax.ShapeDtypeStruct((TOK, HALF), BF16),
        in_specs=[
            pl.BlockSpec(memory_space=pltpu.SMEM),
            pl.BlockSpec(memory_space=pltpu.VMEM),
            hbm,
        ],
        out_specs=hbm,
        scratch_shapes=[pltpu.SemaphoreType.DMA],
        input_output_aliases={2: 0},
        compiler_params=pltpu.CompilerParams(vmem_limit_bytes=4 << 20),
        name="join",
    )(place, got, half)


def local(item_owner, item_row, seq_lengths, table, w_qkvu, w_out):
    c = lax.axis_index("col")
    swap = [(0, 1), (1, 0)]
    wanted, dest = route(item_owner, item_row)
    asked = lax.all_to_all(wanted[:, None, :], "dp", 0, 0, tiled=True)
    wq1 = lax.ppermute(w_qkvu, "col", swap)
    wo1 = lax.ppermute(w_out, "col", swap)
    place = jnp.reshape(c, (1,)).astype(jnp.int32)
    dest = dest.reshape(TOK)
    asked, wq1, wo1 = lax.optimization_barrier((asked, wq1, wo1))
    fetched = fetch(asked[:, 0, :], table)
    arrived = lax.all_to_all(fetched.reshape(128, 4 * CAP, 128), "dp", 0, 0, tiled=True)
    mine, send, held = put(place, dest, arrived.reshape(128 * 4 * CAP, 128), wq1)
    theirs = lax.ppermute(send, "col", swap)
    out, hidden = layer(place, seq_lengths, mine, theirs, w_qkvu, held, w_out, wo1)
    got = lax.ppermute(out, "col", swap)
    half = keep(place, hidden, mine, w_out, wo1)
    return join(place, got, half)


def solution(mesh):
    return jax.shard_map(
        local,
        mesh=mesh,
        in_specs=(
            P("dp", None),
            P("dp"),
            P("dp", None),
            P("dp", "col"),
            P(None, "col"),
            P("col", None),
        ),
        out_specs=P("dp", "col"),
        check_vma=False,
    )
```

```python
import jax
import jax.numpy as jnp
from jax import lax
from jax.experimental import pallas as pl
from jax.experimental.pallas import tpu as pltpu
from jax.sharding import PartitionSpec as P

D = 1024
DH = 128
MAX_LEN = 256
TOK = 1024
HALF = 512
CAP = 10
WIN = HALF + MAX_LEN
LOCAL = 4
F32 = jnp.float32
BF16 = jnp.bfloat16
NT = (((1,), (1,)), ((), ()))


def route_kernel(owner_ref, row_ref, wanted_ref, dest_ref):
    blocks = TOK // 128
    sub = lax.broadcasted_iota(jnp.int32, (128, 128), 0)
    lane = lax.broadcasted_iota(jnp.int32, (128, 128), 1)
    before = (sub < lane).astype(F32).astype(BF16)
    hits = [(sub == owner_ref[b : b + 1, :]).astype(F32) for b in range(blocks)]
    ranks = jnp.dot(
        jnp.concatenate(hits, axis=0).astype(BF16), before, preferred_element_type=F32
    )
    count = jnp.zeros((128, 1), F32)
    kind = lax.broadcasted_iota(jnp.int32, (32, 128), 0)
    values = []
    for b in range(blocks):
        rank = ranks[b * 128 : (b + 1) * 128] + count
        slot = jnp.sum(hits[b] * rank, axis=0, keepdims=True).astype(jnp.int32)
        count = count + jnp.sum(hits[b], axis=1, keepdims=True)
        dest_ref[b : b + 1, :] = owner_ref[b : b + 1, :] * CAP + slot
        row = row_ref[b : b + 1, :]
        spot = ((row >> 3) << 5) + (row & 7)
        part = jnp.where(kind < 16, spot >> 6, spot & 63).astype(F32)
        values.append(jnp.where((kind & 15) == slot, part, 0.0))
    both = lax.dot_general(
        jnp.concatenate(hits, axis=1).astype(BF16),
        jnp.concatenate(values, axis=1).astype(BF16),
        NT,
        preferred_element_type=F32,
    )
    wanted_ref[...] = jnp.zeros((128, 128), jnp.int32)
    wanted_ref[:, :16] = (both[:, :16] * 64.0 + both[:, 16:]).astype(jnp.int32)


def route(owner, row):
    return pl.pallas_call(
        route_kernel,
        out_shape=(
            jax.ShapeDtypeStruct((128, 128), jnp.int32),
            jax.ShapeDtypeStruct((8, 128), jnp.int32),
        ),
        cost_estimate=pl.CostEstimate(
            flops=1 << 32, bytes_accessed=1 << 20, transcendentals=0
        ),
        name="route",
    )(owner.reshape(8, 128), row.reshape(8, 128))


PIECES = 8


def fetch_kernel(asked_ref, table_hbm, out_ref, table_ref, tall_ref, wide_ref, sems):
    rows = 4096 // PIECES
    copies = [
        pltpu.make_async_copy(
            table_hbm.at[pl.ds(i * rows, rows), :],
            table_ref.at[pl.ds(i * rows, rows), :],
            sems.at[i],
        )
        for i in range(PIECES)
    ]
    for cp in copies:
        cp.start()

    def widen(j, _):
        at = pl.ds(pl.multiple_of(j * 16, 16), 16)
        for k in range(4):
            v = table_ref[at, k * 128 : (k + 1) * 128].astype(F32)
            tall_ref[pl.ds(pl.multiple_of(j * 64 + k * 8, 8), 8), :] = v[:8]
            tall_ref[pl.ds(pl.multiple_of(j * 64 + 32 + k * 8, 8), 8), :] = v[8:]
        return 0

    for i in range(PIECES):
        copies[i].wait()
        lax.fori_loop(i * rows // 16, (i + 1) * rows // 16, widen, 0, unroll=4)

    def body(g, _):
        for s in range(CAP):
            at = asked_ref[g, s]
            wide_ref[pl.ds(g * 40 + 4 * s, 4), :] = tall_ref[pl.ds(at, 4, stride=8), :]
        return 0

    lax.fori_loop(0, 128, body, 0, unroll=8)
    out_ref[...] = wide_ref[: 128 * 40, :].astype(BF16)


def fetch(asked, table):
    return pl.pallas_call(
        fetch_kernel,
        out_shape=jax.ShapeDtypeStruct((128 * 40, 128), BF16),
        in_specs=[
            pl.BlockSpec(memory_space=pltpu.SMEM),
            pl.BlockSpec(memory_space=pltpu.HBM),
        ],
        out_specs=pl.BlockSpec(memory_space=pltpu.VMEM),
        scratch_shapes=[
            pltpu.VMEM((4096, HALF), BF16),
            pltpu.VMEM((4096 * 4 + 32, 128), F32),
            pltpu.VMEM((128 * 40 + 8, 128), F32),
            pltpu.SemaphoreType.DMA((PIECES,)),
        ],
        compiler_params=pltpu.CompilerParams(vmem_limit_bytes=60 << 20),
        name="fetch",
    )(asked, table)


def place_kernel(target_ref, dest_ref, arrived_ref, *refs):
    out_ref, wide_ref, emb_ref = refs[-4], refs[-2], refs[-1]
    wide_ref[: 128 * 40, :] = arrived_ref[...].astype(F32)
    base = target_ref[0] * HALF - MAX_LEN

    def body(j, _):
        token = base + j * 8
        token = jnp.where(token < 0, 0, token)
        for r in range(8):
            at = dest_ref[token + r]
            emb_ref[pl.ds(j * 32 + r, 4, stride=8), :] = wide_ref[
                pl.ds(pl.multiple_of(at * 4, 4), 4), :
            ]
        return 0

    lax.fori_loop(0, WIN // 8, body, 0, unroll=2)

    def pack(m, _):
        rows = pl.ds(pl.multiple_of(m * 16, 16), 16)
        for k in range(4):
            lo = emb_ref[pl.ds(pl.multiple_of(m * 64 + k * 8, 8), 8), :]
            hi = emb_ref[pl.ds(pl.multiple_of(m * 64 + 32 + k * 8, 8), 8), :]
            out_ref[rows, k * 128 : (k + 1) * 128] = jnp.concatenate([lo, hi], axis=0).astype(BF16)
        return 0

    lax.fori_loop(0, WIN // 16, pack, 0, unroll=4)


def put(target, dest, arrived, w):
    vmem = pl.BlockSpec(memory_space=pltpu.VMEM)
    smem = pl.BlockSpec(memory_space=pltpu.SMEM)
    hbm = pl.BlockSpec(memory_space=pltpu.HBM)
    return pl.pallas_call(
        place_kernel,
        out_shape=(
            jax.ShapeDtypeStruct((WIN, HALF), BF16),
            jax.ShapeDtypeStruct((D, 4 * HALF), BF16),
        ),
        in_specs=[smem, smem, vmem, hbm],
        out_specs=(vmem, hbm),
        input_output_aliases={3: 1},
        scratch_shapes=[
            pltpu.VMEM((128 * 40 + 8, 128), F32),
            pltpu.VMEM((WIN * 4 + 32, 128), F32),
        ],
        compiler_params=pltpu.CompilerParams(vmem_limit_bytes=12 << 20),
        cost_estimate=pl.CostEstimate(
            flops=1 << 20, bytes_accessed=6 << 20, transcendentals=0
        ),
        name="put",
    )(target, dest, arrived, w)


def silu(x):
    h = x * F32(0.5)
    return h * (F32(1.0) + jnp.tanh(h))


def layer_kernel(
    place_ref,
    lengths_ref,
    mine_ref,
    theirs_ref,
    wq0_ref,
    wq1_hbm,
    wo0_hbm,
    wo1_hbm,
    send_ref,
    hidden_ref,
    kv_ref,
    qu_ref,
    emb_ref,
    w_ref,
    wo_ref,
    mask_ref,
    attn_ref,
    gate_ref,
    sems,
):
    c = place_ref[0]
    other = pl.multiple_of(HALF - c * HALF, HALF)
    copies = [
        pltpu.make_async_copy(
            wq1_hbm.at[:, pl.ds(h * 512, 512)], w_ref.at[h], sems.at[h]
        )
        for h in range(LOCAL)
    ]
    for part, src in enumerate((wo0_hbm, wo1_hbm)):
        copies.append(
            pltpu.make_async_copy(
                src.at[:, pl.ds(other, HALF)],
                wo_ref.at[pl.ds(part * HALF, HALF)],
                sems.at[LOCAL + part],
            )
        )
    for cp in copies:
        cp.start()

    @pl.when(c == 0)
    def _():
        emb_ref[:, :HALF] = mine_ref[...]
        emb_ref[:, HALF:] = theirs_ref[...]

    @pl.when(c != 0)
    def _():
        emb_ref[:, :HALF] = theirs_ref[...]
        emb_ref[:, HALF:] = mine_ref[...]

    base = c * HALF - MAX_LEN
    for b in range(2):
        q = lax.broadcasted_iota(jnp.int32, (256, 1), 0) + (base + 256 * (b + 1))
        k = lax.broadcasted_iota(jnp.int32, (256, 512), 1) + (base + 256 * b)
        first = jnp.zeros((256, 1), jnp.int32)
        end = jnp.int32(0)
        for s in range(8):
            end = end + lengths_ref[0, s]
            first = jnp.where(q >= end, end, first)
        ok = (k >= first) & (k <= q)
        mask_ref[b] = jnp.where(ok, F32(1.0 / MAX_LEN), F32(0.0))

    scale = F32(0.5 / (DH**0.5))
    def attend(n, qu, kv):
        for b in range(2):
            ks = kv[b * 256 : b * 256 + 512, :DH]
            vs = kv[b * 256 : b * 256 + 512, DH:]
            s = lax.dot_general(
                qu[b * 256 : (b + 1) * 256, :DH], ks, NT, preferred_element_type=F32
            )
            h = s * scale
            p = (h * (F32(1.0) + jnp.tanh(h)) * mask_ref[b]).astype(BF16)
            attn_ref[b * 256 : (b + 1) * 256, n * DH : (n + 1) * DH] = jnp.dot(
                p, vs, preferred_element_type=F32
            )

    for n in range(9):
        if n < 8:
            if n < LOCAL:
                w = wq0_ref.at[:, n * 512 : (n + 1) * 512]
            else:
                copies[n - LOCAL].wait()
                w = w_ref.at[n - LOCAL]
            kv_ref[n % 2] = silu(
                jnp.dot(emb_ref[...], w[:, DH : 3 * DH], preferred_element_type=F32)
            ).astype(BF16)
        if n > 0:
            attend(n - 1, qu_ref[(n - 1) % 2], kv_ref[(n - 1) % 2])
        if n < 8:
            ends = jnp.concatenate([w[:, :DH], w[:, 3 * DH :]], axis=1)
            qu = silu(
                jnp.dot(emb_ref[MAX_LEN:, :], ends, preferred_element_type=F32)
            ).astype(BF16)
            qu_ref[n % 2] = qu
            gate_ref[:, n * DH : (n + 1) * DH] = qu[:, DH:]
    copies[LOCAL].wait()
    copies[LOCAL + 1].wait()
    for b in range(2):
        at = slice(b * 256, (b + 1) * 256)
        attn = attn_ref[at, :]
        mean = jnp.sum(attn, axis=1, keepdims=True) * F32(1.0 / D)
        msq = jnp.sum(attn * attn, axis=1, keepdims=True) * F32(1.0 / D)
        scale_row = lax.rsqrt(msq - mean * mean + F32(1e-05))
        hidden = ((attn - mean) * scale_row * gate_ref[at, :].astype(F32)).astype(BF16)
        hidden_ref[at, :] = hidden
        mixed = jnp.dot(hidden, wo_ref[...], preferred_element_type=F32)
        emb = theirs_ref[MAX_LEN + b * 256 : MAX_LEN + (b + 1) * 256, :].astype(F32)
        send_ref[at, :] = (emb + mixed).astype(BF16)


def layer(place, lengths, mine, theirs, wq0, wq1, wo0, wo1):
    vmem = pl.BlockSpec(memory_space=pltpu.VMEM)
    hbm = pl.BlockSpec(memory_space=pltpu.HBM)
    smem = pl.BlockSpec(memory_space=pltpu.SMEM)
    return pl.pallas_call(
        layer_kernel,
        out_shape=(
            jax.ShapeDtypeStruct((HALF, HALF), BF16),
            jax.ShapeDtypeStruct((HALF, D), BF16),
        ),
        in_specs=[smem, smem, vmem, vmem, vmem] + [hbm] * 3,
        out_specs=(vmem, vmem),
        scratch_shapes=[
            pltpu.VMEM((2, WIN, 256), BF16),
            pltpu.VMEM((2, HALF, 256), BF16),
            pltpu.VMEM((WIN, D), BF16),
            pltpu.VMEM((LOCAL, D, 512), BF16),
            pltpu.VMEM((D, HALF), BF16),
            pltpu.VMEM((2, 256, 512), F32),
            pltpu.VMEM((HALF, D), F32),
            pltpu.VMEM((HALF, D), BF16),
            pltpu.SemaphoreType.DMA((LOCAL + 2,)),
        ],
        compiler_params=pltpu.CompilerParams(vmem_limit_bytes=30 << 20),
        cost_estimate=pl.CostEstimate(
            flops=7 << 30, bytes_accessed=12 << 20, transcendentals=5 << 20
        ),
        name="layer",
    )(place, lengths, mine, theirs, wq0, wq1, wo0, wo1)


def keep_kernel(
    place_ref, hidden_ref, mine_ref, wo0_hbm, wo1_hbm, out_hbm, wo_ref, out_ref, sems
):
    mine = pl.multiple_of(place_ref[0] * HALF, HALF)
    copies = [
        pltpu.make_async_copy(
            src.at[:, pl.ds(mine, HALF)], wo_ref.at[pl.ds(part * HALF, HALF)], sems.at[part]
        )
        for part, src in enumerate((wo0_hbm, wo1_hbm))
    ]
    for cp in copies:
        cp.start()
    for cp in copies:
        cp.wait()
    mixed = jnp.dot(hidden_ref[...], wo_ref[...], preferred_element_type=F32)
    out_ref[...] = (mine_ref[MAX_LEN:, :].astype(F32) + mixed).astype(BF16)
    done = pltpu.make_async_copy(out_ref, out_hbm.at[pl.ds(mine, HALF), :], sems.at[2])
    done.start()
    done.wait()


def keep(place, hidden, mine, wo0, wo1):
    vmem = pl.BlockSpec(memory_space=pltpu.VMEM)
    hbm = pl.BlockSpec(memory_space=pltpu.HBM)
    return pl.pallas_call(
        keep_kernel,
        out_shape=jax.ShapeDtypeStruct((TOK, HALF), BF16),
        in_specs=[pl.BlockSpec(memory_space=pltpu.SMEM), vmem, vmem, hbm, hbm],
        out_specs=hbm,
        scratch_shapes=[
            pltpu.VMEM((D, HALF), BF16),
            pltpu.VMEM((HALF, HALF), BF16),
            pltpu.SemaphoreType.DMA((3,)),
        ],
        compiler_params=pltpu.CompilerParams(vmem_limit_bytes=10 << 20),
        cost_estimate=pl.CostEstimate(
            flops=1 << 29, bytes_accessed=3 << 20, transcendentals=0
        ),
        name="keep",
    )(place, hidden, mine, wo0, wo1)


def join_kernel(place_ref, got_ref, half_hbm, out_hbm, sem):
    other = pl.multiple_of(HALF - place_ref[0] * HALF, HALF)
    done = pltpu.make_async_copy(got_ref, out_hbm.at[pl.ds(other, HALF), :], sem)
    done.start()
    done.wait()


def join(place, got, half):
    hbm = pl.BlockSpec(memory_space=pltpu.HBM)
    return pl.pallas_call(
        join_kernel,
        out_shape=jax.ShapeDtypeStruct((TOK, HALF), BF16),
        in_specs=[
            pl.BlockSpec(memory_space=pltpu.SMEM),
            pl.BlockSpec(memory_space=pltpu.VMEM),
            hbm,
        ],
        out_specs=hbm,
        scratch_shapes=[pltpu.SemaphoreType.DMA],
        input_output_aliases={2: 0},
        compiler_params=pltpu.CompilerParams(vmem_limit_bytes=4 << 20),
        name="join",
    )(place, got, half)


def local(item_owner, item_row, seq_lengths, table, w_qkvu, w_out):
    c = lax.axis_index("col")
    swap = [(0, 1), (1, 0)]
    wanted, dest = route(item_owner, item_row)
    asked = lax.all_to_all(wanted[:, None, :], "dp", 0, 0, tiled=True)
    wq1 = lax.ppermute(w_qkvu, "col", swap)
    wo1 = lax.ppermute(w_out, "col", swap)
    place = jnp.reshape(c, (1,)).astype(jnp.int32)
    dest = dest.reshape(TOK)
    asked, wq1, wo1 = lax.optimization_barrier((asked, wq1, wo1))
    fetched = fetch(asked[:, 0, :], table)
    arrived = lax.all_to_all(fetched.reshape(128, 4 * CAP, 128), "dp", 0, 0, tiled=True)
    arrived = arrived.reshape(128 * 4 * CAP, 128)
    send, held = put(1 - place, dest, arrived, wq1)
    theirs = lax.ppermute(send, "col", swap)
    mine, held = put(place, dest, arrived, held)
    out, hidden = layer(place, seq_lengths, mine, theirs, w_qkvu, held, w_out, wo1)
    got = lax.ppermute(out, "col", swap)
    half = keep(place, hidden, mine, w_out, wo1)
    return join(place, got, half)


def solution(mesh):
    return jax.shard_map(
        local,
        mesh=mesh,
        in_specs=(
            P("dp", None),
            P("dp"),
            P("dp", None),
            P("dp", "col"),
            P(None, "col"),
            P("col", None),
        ),
        out_specs=P("dp", "col"),
        check_vma=False,
    )
```

```python
import jax
import jax.numpy as jnp
from jax import lax
from jax.experimental import pallas as pl
from jax.experimental.pallas import tpu as pltpu
from jax.sharding import PartitionSpec as P

D = 1024
DH = 128
MAX_LEN = 256
TOK = 1024
HALF = 512
CAP = 10
WIN = HALF + MAX_LEN
LOCAL = 4
F32 = jnp.float32
BF16 = jnp.bfloat16
NT = (((1,), (1,)), ((), ()))


def route_kernel(owner_ref, row_ref, wanted_ref, dest_ref):
    blocks = TOK // 128
    sub = lax.broadcasted_iota(jnp.int32, (128, 128), 0)
    lane = lax.broadcasted_iota(jnp.int32, (128, 128), 1)
    before = (sub < lane).astype(F32).astype(BF16)
    hits = [(sub == owner_ref[b : b + 1, :]).astype(F32) for b in range(blocks)]
    ranks = jnp.dot(
        jnp.concatenate(hits, axis=0).astype(BF16), before, preferred_element_type=F32
    )
    count = jnp.zeros((128, 1), F32)
    kind = lax.broadcasted_iota(jnp.int32, (32, 128), 0)
    values = []
    for b in range(blocks):
        rank = ranks[b * 128 : (b + 1) * 128] + count
        slot = jnp.sum(hits[b] * rank, axis=0, keepdims=True).astype(jnp.int32)
        count = count + jnp.sum(hits[b], axis=1, keepdims=True)
        dest_ref[b : b + 1, :] = owner_ref[b : b + 1, :] * CAP + slot
        row = row_ref[b : b + 1, :]
        spot = ((row >> 3) << 5) + (row & 7)
        part = jnp.where(kind < 16, spot >> 6, spot & 63).astype(F32)
        values.append(jnp.where((kind & 15) == slot, part, 0.0))
    both = lax.dot_general(
        jnp.concatenate(hits, axis=1).astype(BF16),
        jnp.concatenate(values, axis=1).astype(BF16),
        NT,
        preferred_element_type=F32,
    )
    wanted_ref[...] = jnp.zeros((128, 128), jnp.int32)
    wanted_ref[:, :16] = (both[:, :16] * 64.0 + both[:, 16:]).astype(jnp.int32)


def route(owner, row):
    return pl.pallas_call(
        route_kernel,
        out_shape=(
            jax.ShapeDtypeStruct((128, 128), jnp.int32),
            jax.ShapeDtypeStruct((8, 128), jnp.int32),
        ),
        cost_estimate=pl.CostEstimate(
            flops=1 << 32, bytes_accessed=1 << 20, transcendentals=0
        ),
        name="route",
    )(owner.reshape(8, 128), row.reshape(8, 128))


PIECES = 8


def fetch_kernel(
    asked_hbm, table_hbm, out_ref, asked_ref, table_ref, tall_ref, wide_ref, sems
):
    rows = 4096 // PIECES
    copies = [
        pltpu.make_async_copy(
            table_hbm.at[pl.ds(i * rows, rows), :],
            table_ref.at[pl.ds(i * rows, rows), :],
            sems.at[i],
        )
        for i in range(PIECES)
    ]
    for cp in copies:
        cp.start()
    listing = pltpu.make_async_copy(asked_hbm, asked_ref, sems.at[PIECES])
    listing.start()

    def widen(j, _):
        at = pl.ds(pl.multiple_of(j * 16, 16), 16)
        for k in range(4):
            v = table_ref[at, k * 128 : (k + 1) * 128].astype(F32)
            tall_ref[pl.ds(pl.multiple_of(j * 64 + k * 8, 8), 8), :] = v[:8]
            tall_ref[pl.ds(pl.multiple_of(j * 64 + 32 + k * 8, 8), 8), :] = v[8:]
        return 0

    for i in range(PIECES):
        copies[i].wait()
        lax.fori_loop(i * rows // 16, (i + 1) * rows // 16, widen, 0, unroll=8)

    listing.wait()

    def body(g, _):
        for s in range(CAP):
            at = asked_ref[g, s]
            wide_ref[pl.ds(g * 40 + 4 * s, 4), :] = tall_ref[pl.ds(at, 4, stride=8), :]
        return 0

    lax.fori_loop(0, 128, body, 0, unroll=16)
    out_ref[...] = wide_ref[: 128 * 40, :].astype(BF16)


def fetch(asked, table):
    return pl.pallas_call(
        fetch_kernel,
        out_shape=jax.ShapeDtypeStruct((128 * 40, 128), BF16),
        in_specs=[
            pl.BlockSpec(memory_space=pltpu.HBM),
            pl.BlockSpec(memory_space=pltpu.HBM),
        ],
        out_specs=pl.BlockSpec(memory_space=pltpu.VMEM),
        scratch_shapes=[
            pltpu.SMEM((128, 128), jnp.int32),
            pltpu.VMEM((4096, HALF), BF16),
            pltpu.VMEM((4096 * 4 + 32, 128), F32),
            pltpu.VMEM((128 * 40 + 8, 128), F32),
            pltpu.SemaphoreType.DMA((PIECES + 1,)),
        ],
        compiler_params=pltpu.CompilerParams(vmem_limit_bytes=60 << 20),
        name="fetch",
    )(asked, table)


def place_kernel(target_ref, dest_ref, arrived_ref, *refs):
    out_ref, wide_ref, emb_ref = refs[-4], refs[-2], refs[-1]
    wide_ref[: 128 * 40, :] = arrived_ref[...].astype(F32)
    base = target_ref[0] * HALF - MAX_LEN

    def body(j, _):
        token = base + j * 8
        token = jnp.where(token < 0, 0, token)
        for r in range(8):
            at = dest_ref[token + r]
            emb_ref[pl.ds(j * 32 + r, 4, stride=8), :] = wide_ref[
                pl.ds(pl.multiple_of(at * 4, 4), 4), :
            ]
        return 0

    lax.fori_loop(0, WIN // 8, body, 0, unroll=8)

    def pack(m, _):
        rows = pl.ds(pl.multiple_of(m * 16, 16), 16)
        for k in range(4):
            lo = emb_ref[pl.ds(pl.multiple_of(m * 64 + k * 8, 8), 8), :]
            hi = emb_ref[pl.ds(pl.multiple_of(m * 64 + 32 + k * 8, 8), 8), :]
            out_ref[rows, k * 128 : (k + 1) * 128] = jnp.concatenate([lo, hi], axis=0).astype(BF16)
        return 0

    lax.fori_loop(0, WIN // 16, pack, 0, unroll=8)


def put(target, dest, arrived, w):
    vmem = pl.BlockSpec(memory_space=pltpu.VMEM)
    smem = pl.BlockSpec(memory_space=pltpu.SMEM)
    hbm = pl.BlockSpec(memory_space=pltpu.HBM)
    return pl.pallas_call(
        place_kernel,
        out_shape=(
            jax.ShapeDtypeStruct((WIN, HALF), BF16),
            jax.ShapeDtypeStruct((D, 4 * HALF), BF16),
        ),
        in_specs=[smem, smem, vmem, hbm],
        out_specs=(vmem, hbm),
        input_output_aliases={3: 1},
        scratch_shapes=[
            pltpu.VMEM((128 * 40 + 8, 128), F32),
            pltpu.VMEM((WIN * 4 + 32, 128), F32),
        ],
        compiler_params=pltpu.CompilerParams(vmem_limit_bytes=12 << 20),
        cost_estimate=pl.CostEstimate(
            flops=1 << 20, bytes_accessed=6 << 20, transcendentals=0
        ),
        name="put",
    )(target, dest, arrived, w)


def silu(x):
    h = x * F32(0.5)
    return h * (F32(1.0) + jnp.tanh(h))


def layer_kernel(
    place_ref,
    lengths_ref,
    mine_ref,
    theirs_ref,
    wq0_ref,
    wq1_hbm,
    wo0_hbm,
    wo1_hbm,
    send_ref,
    hidden_ref,
    kv_ref,
    qu_ref,
    emb_ref,
    w_ref,
    wo_ref,
    mask_ref,
    attn_ref,
    gate_ref,
    sems,
):
    c = place_ref[0]
    other = pl.multiple_of(HALF - c * HALF, HALF)
    copies = [
        pltpu.make_async_copy(
            wq1_hbm.at[:, pl.ds(h * 512, 512)], w_ref.at[h], sems.at[h]
        )
        for h in range(LOCAL)
    ]
    for part, src in enumerate((wo0_hbm, wo1_hbm)):
        copies.append(
            pltpu.make_async_copy(
                src.at[:, pl.ds(other, HALF)],
                wo_ref.at[pl.ds(part * HALF, HALF)],
                sems.at[LOCAL + part],
            )
        )
    for cp in copies:
        cp.start()

    @pl.when(c == 0)
    def _():
        emb_ref[:, :HALF] = mine_ref[...]
        emb_ref[:, HALF:] = theirs_ref[...]

    @pl.when(c != 0)
    def _():
        emb_ref[:, :HALF] = theirs_ref[...]
        emb_ref[:, HALF:] = mine_ref[...]

    base = c * HALF - MAX_LEN
    for b in range(2):
        q = lax.broadcasted_iota(jnp.int32, (256, 1), 0) + (base + 256 * (b + 1))
        k = lax.broadcasted_iota(jnp.int32, (256, 512), 1) + (base + 256 * b)
        first = jnp.zeros((256, 1), jnp.int32)
        end = jnp.int32(0)
        for s in range(8):
            end = end + lengths_ref[0, s]
            first = jnp.where(q >= end, end, first)
        ok = (k >= first) & (k <= q)
        mask_ref[b] = jnp.where(ok, F32(1.0 / MAX_LEN), F32(0.0))

    scale = F32(0.5 / (DH**0.5))
    def attend(n, qu, kv):
        for b in range(2):
            ks = kv[b * 256 : b * 256 + 512, :DH]
            vs = kv[b * 256 : b * 256 + 512, DH:]
            s = lax.dot_general(
                qu[b * 256 : (b + 1) * 256, :DH], ks, NT, preferred_element_type=F32
            )
            h = s * scale
            p = (h * (F32(1.0) + jnp.tanh(h)) * mask_ref[b]).astype(BF16)
            attn_ref[b * 256 : (b + 1) * 256, n * DH : (n + 1) * DH] = jnp.dot(
                p, vs, preferred_element_type=F32
            )

    for n in range(9):
        if n < 8:
            if n < LOCAL:
                w = wq0_ref.at[:, n * 512 : (n + 1) * 512]
            else:
                copies[n - LOCAL].wait()
                w = w_ref.at[n - LOCAL]
            kv_ref[n % 2] = silu(
                jnp.dot(emb_ref[...], w[:, DH : 3 * DH], preferred_element_type=F32)
            ).astype(BF16)
        if n > 0:
            attend(n - 1, qu_ref[(n - 1) % 2], kv_ref[(n - 1) % 2])
        if n < 8:
            ends = jnp.concatenate([w[:, :DH], w[:, 3 * DH :]], axis=1)
            qu = silu(
                jnp.dot(emb_ref[MAX_LEN:, :], ends, preferred_element_type=F32)
            ).astype(BF16)
            qu_ref[n % 2] = qu
            gate_ref[:, n * DH : (n + 1) * DH] = qu[:, DH:]
    copies[LOCAL].wait()
    copies[LOCAL + 1].wait()
    for b in range(2):
        at = slice(b * 256, (b + 1) * 256)
        attn = attn_ref[at, :]
        mean = jnp.sum(attn, axis=1, keepdims=True) * F32(1.0 / D)
        msq = jnp.sum(attn * attn, axis=1, keepdims=True) * F32(1.0 / D)
        scale_row = lax.rsqrt(msq - mean * mean + F32(1e-05))
        hidden = ((attn - mean) * scale_row * gate_ref[at, :].astype(F32)).astype(BF16)
        hidden_ref[at, :] = hidden
        mixed = jnp.dot(hidden, wo_ref[...], preferred_element_type=F32)
        emb = theirs_ref[MAX_LEN + b * 256 : MAX_LEN + (b + 1) * 256, :].astype(F32)
        send_ref[at, :] = (emb + mixed).astype(BF16)


def layer(place, lengths, mine, theirs, wq0, wq1, wo0, wo1):
    vmem = pl.BlockSpec(memory_space=pltpu.VMEM)
    hbm = pl.BlockSpec(memory_space=pltpu.HBM)
    smem = pl.BlockSpec(memory_space=pltpu.SMEM)
    return pl.pallas_call(
        layer_kernel,
        out_shape=(
            jax.ShapeDtypeStruct((HALF, HALF), BF16),
            jax.ShapeDtypeStruct((HALF, D), BF16),
        ),
        in_specs=[smem, smem, vmem, vmem, vmem] + [hbm] * 3,
        out_specs=(vmem, vmem),
        scratch_shapes=[
            pltpu.VMEM((2, WIN, 256), BF16),
            pltpu.VMEM((2, HALF, 256), BF16),
            pltpu.VMEM((WIN, D), BF16),
            pltpu.VMEM((LOCAL, D, 512), BF16),
            pltpu.VMEM((D, HALF), BF16),
            pltpu.VMEM((2, 256, 512), F32),
            pltpu.VMEM((HALF, D), F32),
            pltpu.VMEM((HALF, D), BF16),
            pltpu.SemaphoreType.DMA((LOCAL + 2,)),
        ],
        compiler_params=pltpu.CompilerParams(vmem_limit_bytes=30 << 20),
        cost_estimate=pl.CostEstimate(
            flops=7 << 30, bytes_accessed=12 << 20, transcendentals=5 << 20
        ),
        name="layer",
    )(place, lengths, mine, theirs, wq0, wq1, wo0, wo1)


def keep_kernel(
    place_ref, hidden_ref, mine_ref, wo0_hbm, wo1_hbm, out_hbm, wo_ref, out_ref, sems
):
    mine = pl.multiple_of(place_ref[0] * HALF, HALF)
    copies = [
        pltpu.make_async_copy(
            src.at[:, pl.ds(mine, HALF)], wo_ref.at[pl.ds(part * HALF, HALF)], sems.at[part]
        )
        for part, src in enumerate((wo0_hbm, wo1_hbm))
    ]
    for cp in copies:
        cp.start()
    for cp in copies:
        cp.wait()
    mixed = jnp.dot(hidden_ref[...], wo_ref[...], preferred_element_type=F32)
    out_ref[...] = (mine_ref[MAX_LEN:, :].astype(F32) + mixed).astype(BF16)
    done = pltpu.make_async_copy(out_ref, out_hbm.at[pl.ds(mine, HALF), :], sems.at[2])
    done.start()
    done.wait()


def keep(place, hidden, mine, wo0, wo1):
    vmem = pl.BlockSpec(memory_space=pltpu.VMEM)
    hbm = pl.BlockSpec(memory_space=pltpu.HBM)
    return pl.pallas_call(
        keep_kernel,
        out_shape=jax.ShapeDtypeStruct((TOK, HALF), BF16),
        in_specs=[pl.BlockSpec(memory_space=pltpu.SMEM), vmem, vmem, hbm, hbm],
        out_specs=hbm,
        scratch_shapes=[
            pltpu.VMEM((D, HALF), BF16),
            pltpu.VMEM((HALF, HALF), BF16),
            pltpu.SemaphoreType.DMA((3,)),
        ],
        compiler_params=pltpu.CompilerParams(vmem_limit_bytes=10 << 20),
        cost_estimate=pl.CostEstimate(
            flops=1 << 29, bytes_accessed=3 << 20, transcendentals=0
        ),
        name="keep",
    )(place, hidden, mine, wo0, wo1)


def join_kernel(place_ref, got_ref, half_hbm, out_hbm, sem):
    other = pl.multiple_of(HALF - place_ref[0] * HALF, HALF)
    done = pltpu.make_async_copy(got_ref, out_hbm.at[pl.ds(other, HALF), :], sem)
    done.start()
    done.wait()


def join(place, got, half):
    hbm = pl.BlockSpec(memory_space=pltpu.HBM)
    return pl.pallas_call(
        join_kernel,
        out_shape=jax.ShapeDtypeStruct((TOK, HALF), BF16),
        in_specs=[
            pl.BlockSpec(memory_space=pltpu.SMEM),
            pl.BlockSpec(memory_space=pltpu.VMEM),
            hbm,
        ],
        out_specs=hbm,
        scratch_shapes=[pltpu.SemaphoreType.DMA],
        input_output_aliases={2: 0},
        compiler_params=pltpu.CompilerParams(vmem_limit_bytes=4 << 20),
        name="join",
    )(place, got, half)


def local(item_owner, item_row, seq_lengths, table, w_qkvu, w_out):
    c = lax.axis_index("col")
    swap = [(0, 1), (1, 0)]
    wanted, dest = route(item_owner, item_row)
    asked = lax.all_to_all(wanted[:, None, :], "dp", 0, 0, tiled=True)
    wq1 = lax.ppermute(w_qkvu, "col", swap)
    wo1 = lax.ppermute(w_out, "col", swap)
    place = jnp.reshape(c, (1,)).astype(jnp.int32)
    dest = dest.reshape(TOK)
    asked, wq1, wo1 = lax.optimization_barrier((asked, wq1, wo1))
    fetched = fetch(asked[:, 0, :], table)
    arrived = lax.all_to_all(fetched.reshape(128, 4 * CAP, 128), "dp", 0, 0, tiled=True)
    arrived = arrived.reshape(128 * 4 * CAP, 128)
    send, held = put(1 - place, dest, arrived, wq1)
    theirs = lax.ppermute(send, "col", swap)
    mine, held = put(place, dest, arrived, held)
    out, hidden = layer(place, seq_lengths, mine, theirs, w_qkvu, held, w_out, wo1)
    got = lax.ppermute(out, "col", swap)
    half = keep(place, hidden, mine, w_out, wo1)
    return join(place, got, half)


def solution(mesh):
    return jax.shard_map(
        local,
        mesh=mesh,
        in_specs=(
            P("dp", None),
            P("dp"),
            P("dp", None),
            P("dp", "col"),
            P(None, "col"),
            P("col", None),
        ),
        out_specs=P("dp", "col"),
        check_vma=False,
    )
```
